256 devices in a mesh: row: 16 (over z, y_lo), col: 16 (over y_hi, x, core).
Axes of the slice: x: 4, y: 4 (y_hi: 2, y_lo: 2; y = y_hi * 2 + y_lo), z: 8, core: 2. Of those that a mesh axis runs over, the one named last changes fastest.
Arguments:
- ancestor: float32 [8192, 8192], P('row', 'col'), may hold values from -0.0625 to 0.0625
- factor: float32 [8192, 16, 128], P(('row', 'col')), may hold values from -1.5 to 1.5
- diag_inv: float32 [16, 128, 128], replicated, may hold values from -6 to 6
- structure: int32 [16, 768], replicated, may hold values from 0 to 1023, as said below
Outputs:
- inverse_panel: float32 [8192, 16, 128], P(('row', 'col'))
- inverse_diagonal: float32 [16, 128, 128], replicated
The draws below stay inside these ranges and needn't reach their ends.
Inputs may be any that keep to these rules, and one draw needn't show every extreme that they name: Each row of structure lists 768 different block numbers, in no particular order.
All inputs are finite; a program needn't handle non-finite values.
Results may differ from the reference program's by a relative error of at most 0.00007.
Values sent between devices are 32-bit elements; how exact they have to be, the bound alone decides.
No kernel may reach another device: no remote copies, remote signals or barrier semaphores. Data moves between devices by JAX's collectives and lax.ppermute only.
A program may use at most 64 MiB of HBM per device.

```python
import jax
import jax.numpy as jnp
from jax import lax

W = 128
SIB = 16
RB = 8
NA = 8192
NBLK = 1024
NSEL = 768


def draw_structure(key, part):
    sibling_keys = jax.random.split(jax.random.fold_in(key, 11), SIB)
    orders = jax.vmap(lambda single_key: jax.random.permutation(single_key, NBLK))(sibling_keys)
    return orders[:, :NSEL].astype(jnp.int32)


def block_scale(own_key, extent, cuts, low, high):
    def one(axis_at, parts):
        steps = jax.random.uniform(jax.random.fold_in(jax.random.fold_in(own_key, 6), axis_at), (parts,), jnp.float32, low / len(cuts), high / len(cuts))
        return jnp.repeat(jnp.exp(steps), extent[axis_at] // parts).reshape((-1,) + (1,) * (len(extent) - axis_at - 1))

    gain = one(*cuts[0])
    for cut in cuts[1:]:
        gain = gain * one(*cut)
    return gain


def bell_draw(key, dims, spread, limit, pieces=(), held_as=jnp.bfloat16):
    loudness = block_scale(key, dims, pieces, -0.22, 0.18) if pieces else 1.0
    values = jax.random.normal(key, dims, jnp.float32) * spread * loudness
    return jnp.minimum(jnp.maximum(values, -limit), limit).astype(held_as)


def setup_inputs(seed: int = 0) -> dict:
    keys = jax.random.split(jax.random.key(seed), 5)
    ancestor = bell_draw(keys[0], (NA, NA), NA ** -0.5, 0.0625, ((0, 16), (1, 16)), jnp.float32)
    factor = bell_draw(keys[1], (NA, SIB, W), 0.25, 1.5, ((0, 256),), jnp.float32)
    diag_inv = bell_draw(keys[2], (SIB, W, W), 1.0, 6.0, (), jnp.float32)
    structure = draw_structure(jax.random.fold_in(keys[4], 71), 0)
    return {"ancestor": ancestor, "factor": factor, "diag_inv": diag_inv, "structure": structure}


def reference(ancestor, factor, diag_inv, structure):
    sibling_ids = jnp.arange(SIB, dtype=jnp.int32)[:, None]
    block_mask = jnp.zeros((SIB, NBLK), jnp.float32).at[sibling_ids, structure].set(1.0)
    row_mask = jnp.repeat(block_mask, RB, axis=1).T
    masked = factor * row_mask[:, :, None]
    product = jnp.dot(ancestor, masked.reshape(NA, SIB * W), precision=lax.Precision.HIGHEST, preferred_element_type=jnp.float32)
    panel = -product.reshape(NA, SIB, W) * row_mask[:, :, None]
    update = jnp.einsum("bsw,bsv->swv", masked, panel, precision=lax.Precision.HIGHEST)
    return panel, diag_inv - update
```

```python
import jax
import jax.numpy as jnp
from jax import lax
from jax.sharding import Mesh, PartitionSpec as P

RB = 8
AXES = ("z", "ylo", "yhi", "x", "core")
ROW = ("z", "ylo")
COL = ("yhi", "x", "core")
QUAD = ("yhi", "x")
GROUP = ("ylo", "core")
NZ, NQ, NG = 8, 8, 4


def shift(count, step):
    return [(i, (i + step) % count) for i in range(count)]


def swap(value, axis):
    return lax.ppermute(value, axis, [(0, 1), (1, 0)])


def group_exchange(pieces, group):
    out = jnp.zeros_like(pieces)
    for k in range(NG):
        piece = lax.dynamic_index_in_dim(pieces, group ^ k, 0, keepdims=True)
        if k:
            piece = lax.ppermute(piece, GROUP, [(j, j ^ k) for j in range(NG)])
        out = lax.dynamic_update_slice_in_dim(out, piece, group ^ k, 0)
    return out


def per_device(ancestor, factor, diag_inv, structure):
    rows, sib, width = factor.shape
    cols = sib * width // NG
    half = cols // 2
    z = lax.axis_index("z")
    ylo = lax.axis_index("ylo")
    core = lax.axis_index("core")
    group = ylo * 2 + core
    first_row = (lax.axis_index(ROW) * (NQ * 2) + lax.axis_index(COL)) * rows
    block_ids = (first_row + jnp.arange(rows, dtype=jnp.int32)) // RB
    matches = block_ids[:, None, None] == structure[None, :, :]
    row_mask = jnp.any(matches, axis=2).astype(jnp.float32)
    masked = factor * row_mask[:, :, None]

    side = ancestor.shape[0]
    tile = ancestor.reshape(NQ, side // NQ, side)
    other = swap(tile, "ylo")
    pair = jnp.where(ylo == 0, jnp.stack([tile, other], 1), jnp.stack([other, tile], 1))
    opposite = swap(pair, "core")
    wide = jnp.where(
        core == 0, jnp.concatenate([pair, opposite], 3), jnp.concatenate([opposite, pair], 3)
    )
    wide = wide.reshape(2 * side, 2 * side)

    flat = masked.reshape(4, 8, NG, 2, half)
    pieces = flat.transpose(0, 3, 2, 1, 4).reshape(NZ * NG, 8, half)
    pieces = lax.all_to_all(pieces, ("z",) + GROUP, 0, 0, tiled=True)
    pieces = pieces.reshape(NZ, 2, 2, 8, half)
    pieces = lax.all_to_all(pieces, QUAD, 0, 0, tiled=True)
    pieces = pieces.transpose(1, 0, 2, 3, 4).reshape(2, NQ, 2, 1, 8, half)

    gathered = jnp.zeros((2, NQ, 2, 4, 8, cols), jnp.float32)

    def place(gathered, piece, source):
        at = source % NZ
        zero = jnp.int32(0)
        return lax.dynamic_update_slice(
            gathered, piece, (zero, zero, zero, at // 2, zero, (at % 2) * half)
        )

    gathered = place(gathered, pieces, z)
    up = down = pieces
    for step in range(1, NZ // 2 + 1):
        up = lax.ppermute(up, "z", shift(NZ, 1))
        if step < NZ // 2:
            down = lax.ppermute(down, "z", shift(NZ, -1))
        gathered = place(gathered, up, z + NZ - step)
        if step < NZ // 2:
            gathered = place(gathered, down, z + step)
    gathered = gathered.reshape(2 * side, cols)

    own = masked.reshape(rows, NG, cols).transpose(1, 0, 2)
    local = group_exchange(own, group)

    partial = jnp.dot(
        wide, gathered, precision=lax.Precision.HIGH, preferred_element_type=jnp.float32
    )
    partial = partial.reshape(NQ, NG * rows, cols)
    product = lax.all_to_all(partial, QUAD, 0, 0, tiled=True).sum(0)

    per = sib // NG
    update = jnp.einsum(
        "bsw,bsv->swv",
        local.reshape(NG * rows, per, width),
        product.reshape(NG * rows, per, width),
        precision=lax.Precision.HIGHEST,
    )
    wide_axes = ("z",) + QUAD
    update = update.reshape(NZ * NQ, per * width // (NZ * NQ), width)
    update = lax.all_to_all(update, wide_axes, 0, 0, tiled=True).sum(0)
    update = jnp.broadcast_to(update[None], (NZ * NQ,) + update.shape)
    update = lax.all_to_all(update, wide_axes, 0, 0, tiled=True)
    update = update.reshape(1, per, width, width)
    other = swap(update, "ylo")
    update = jnp.where(
        ylo == 0, jnp.concatenate([update, other], 0), jnp.concatenate([other, update], 0)
    )
    update = update[:, None]
    other = swap(update, "core")
    update = jnp.where(
        core == 0, jnp.concatenate([update, other], 1), jnp.concatenate([other, update], 1)
    )
    diagonal = diag_inv + update.reshape(sib, width, width)

    back = group_exchange(product.reshape(NG, rows, cols), group)
    panel = back.transpose(1, 0, 2).reshape(rows, sib, width)
    panel = -panel * row_mask[:, :, None]
    return panel, diagonal


def solution(mesh):
    fine = Mesh(mesh.devices.reshape(8, 2, 2, 4, 2), AXES)
    return jax.shard_map(
        per_device,
        mesh=fine,
        in_specs=(P(ROW, COL), P(ROW + COL, None, None), P(), P()),
        out_specs=(P(ROW + COL, None, None), P()),
        check_vma=False,
    )
```

```python
import jax
import jax.numpy as jnp
from jax import lax
from jax.experimental import pallas as pl
from jax.experimental.pallas import tpu as pltpu
from jax.sharding import Mesh, PartitionSpec as P

RB = 8
AXES = ("z", "ylo", "yhi", "x", "core")
ROW = ("z", "ylo")
COL = ("yhi", "x", "core")
RING_Y = ("ylo", "yhi")
GROUP = ("ylo", "yhi", "core")
NZ, NX, NG = 8, 4, 8


def shift(count, step):
    return [(i, (i + step) % count) for i in range(count)]


def flip_to(value, axes, count, bits):
    return lax.ppermute(value, axes, [(j, j ^ bits) for j in range(count)])


def after(value, *others):
    return lax.optimization_barrier((value,) + others)[0]


VMEM = pl.BlockSpec(memory_space=pltpu.VMEM)
SMEM = pl.BlockSpec(memory_space=pltpu.SMEM)


def split(value):
    high = value.astype(jnp.bfloat16)
    return high, (value - high.astype(jnp.float32)).astype(jnp.bfloat16)


def product_kernel(place_ref, *refs):
    blocks, ring, out_ref = refs[:10], refs[10:18], refs[18]
    flat_ref, high_ref, low_ref = refs[19:]
    own, own_c, near, near_c, back, back_c, far0, far0_c, far1, far1_c = blocks
    for k in range(NZ):
        source = lax.bitwise_and(place_ref[5] + (NZ - k), NZ - 1)
        for rel in range(2):
            for yl in range(2):
                tiles = [
                    ring[k][x * 8 + yl * 4 + yh * 2 + c, rel]
                    for yh in range(2)
                    for x in range(NX)
                    for c in range(2)
                ]
                at = rel * 2 + (place_ref[3] ^ yl)
                flat_ref[source & 1, at, :, source >> 1] = jnp.stack(tiles)
    depth = 512
    for i in range(4):
        both = []
        for h in range(2):
            part = flat_ref[h, i]
            both.append(part.reshape(depth, 128))
        high, low = split(jnp.concatenate(both, 1))
        high_ref[i], low_ref[i] = high, low
    for a in range(2):
        for yh in range(2):
            rows = pl.ds(yh * 256, 256)
            if a:
                parts = [near[rows], near_c[rows], back[rows], back_c[rows]]
            else:
                far, far_c = ((far0, far0_c), (far1, far1_c))[yh]
                parts = [own[rows], own_c[rows], far[...], far_c[...]]
            total = jnp.zeros((256, 256), jnp.float32)
            for i, part in enumerate(parts):
                high, low = split(part)
                for left, right in ((high, high_ref), (high, low_ref), (low, high_ref)):
                    total += jnp.dot(left, right[i], preferred_element_type=jnp.float32)
            for x in range(NX):
                out_ref[x, a, yh] = total[x * 64 : (x + 1) * 64]


def product_call(place, blocks, ring, cols):
    return pl.pallas_call(
        product_kernel,
        out_shape=jax.ShapeDtypeStruct((NX, 2, 2, 64, cols), jnp.float32),
        in_specs=[SMEM] + [VMEM] * (len(blocks) + len(ring)),
        out_specs=VMEM,
        scratch_shapes=[
            pltpu.VMEM((2, 4, 16, 4, 8, 128), jnp.float32),
            pltpu.VMEM((4, 512, cols), jnp.bfloat16),
            pltpu.VMEM((4, 512, cols), jnp.bfloat16),
        ],
        compiler_params=pltpu.CompilerParams(vmem_limit_bytes=20 << 20),
        cost_estimate=pl.CostEstimate(
            flops=6 * 1024 * 2048 * 256, bytes_accessed=12 << 20, transcendentals=0
        ),
        name="product",
    )(place, *blocks, *ring)


def pack_kernel(place_ref, factor_ref, structure_ref, pieces_ref, mask_ref, rows_ref, masked_ref):
    structure = structure_ref[...]
    for r in range(4):
        hit = jnp.where(structure == place_ref[0] + r, 1.0, 0.0).astype(jnp.float32)
        mask = jnp.max(hit, axis=1, keepdims=True)
        mask = jnp.broadcast_to(mask, mask_ref.shape[1:])
        mask_ref[r] = mask
        rows = pl.ds(r * 8, 8)
        masked_ref[rows] = factor_ref[rows] * mask[None]
        for s in range(16):
            pieces_ref[r * 2 + s % 2, s // 2] = masked_ref[rows, s, :]
    for s in range(16):
        rows_ref[s // 2, :, pl.ds(s % 2 * 128, 128)] = masked_ref[:, s, :]


def pack_call(place, factor, structure, cols):
    rows, sib, width = factor.shape
    return pl.pallas_call(
        pack_kernel,
        out_shape=[
            jax.ShapeDtypeStruct((NZ, NG, 8, width), jnp.float32),
            jax.ShapeDtypeStruct((4, sib, width), jnp.float32),
            jax.ShapeDtypeStruct((NG, rows, cols), jnp.float32),
        ],
        in_specs=[SMEM, VMEM, VMEM],
        out_specs=[VMEM] * 3,
        scratch_shapes=[pltpu.VMEM((rows, sib, width), jnp.float32)],
        compiler_params=pltpu.CompilerParams(vmem_limit_bytes=4 << 20),
        cost_estimate=pl.CostEstimate(flops=1 << 16, bytes_accessed=1 << 20, transcendentals=0),
        name="pack",
    )(place, factor, structure)


def turn_kernel(in_ref, out_ref):
    for g in range(NG):
        for rel in range(2):
            first = ((g >> 1 & 1) ^ rel) * NX
            out_ref[:, g, rel] = in_ref[first : first + NX, g]


def turn_call(pieces):
    shape = (NX, NG, 2) + pieces.shape[2:]
    return pl.pallas_call(
        turn_kernel,
        out_shape=jax.ShapeDtypeStruct(shape, jnp.float32),
        in_specs=[VMEM],
        out_specs=VMEM,
        compiler_params=pltpu.CompilerParams(vmem_limit_bytes=2 << 20),
        cost_estimate=pl.CostEstimate(flops=0, bytes_accessed=1 << 19, transcendentals=0),
        name="turn",
    )(pieces)


def block_of(place_ref, k):
    return (k >> 2) * 4 + (place_ref[2] ^ (k >> 1 & 1)) * 2 + (place_ref[3] ^ (k & 1))


def reduce_kernel(place_ref, recv_ref, local_ref, *refs):
    update_ref, outs, sum_ref, rows_ref = refs[0], refs[1:5], refs[5], refs[6]
    total = recv_ref[0] + recv_ref[1] + recv_ref[2] + recv_ref[3]
    sum_ref[...] = total.reshape(sum_ref.shape)
    for k in range(NG):
        at = block_of(place_ref, k)
        rows_ref[at] = local_ref[place_ref[1] ^ k]
        for h in range(2):
            outs[k >> 1][1 - k % 2, h] = sum_ref[at, :, pl.ds(h * 128, 128)]
    left = rows_ref[...].reshape(total.shape)
    for s in range(2):
        lanes = slice(s * 128, (s + 1) * 128)
        update_ref[s] = lax.dot_general(
            left[:, lanes],
            total[:, lanes],
            (((0,), (0,)), ((), ())),
            precision=lax.Precision.HIGHEST,
            preferred_element_type=jnp.float32,
        )


def reduce_call(place, recv, local, per, width):
    rows = local.shape[1]
    piece = jax.ShapeDtypeStruct((2, per, rows, width), jnp.float32)
    whole = jax.ShapeDtypeStruct((per, width, width), jnp.float32)
    block = pltpu.VMEM(local.shape, jnp.float32)
    out = pl.pallas_call(
        reduce_kernel,
        out_shape=[whole] + [piece] * 4,
        in_specs=[SMEM, VMEM, VMEM],
        out_specs=[VMEM] * 5,
        scratch_shapes=[block, block],
        compiler_params=pltpu.CompilerParams(vmem_limit_bytes=8 << 20),
        cost_estimate=pl.CostEstimate(flops=1 << 25, bytes_accessed=2 << 20, transcendentals=0),
        name="reduce",
    )(place, recv, local)
    return out[0], out[1:]


def finish_kernel(place_ref, mask_ref, diag_ref, *refs):
    parts, panel_ref, out_ref, flat_ref = refs[:8], refs[8], refs[9], refs[10]
    for c in range(2):
        for k in range(4):
            part = parts[c * 4 + k]
            at = place_ref[1] ^ (k * 2 + c)
            out_ref[at] = diag_ref[at] + part[pl.ds(0, 256)]
            for h in range(2):
                flat_ref[at, h] = part[pl.ds(256 + (1 - c) * 64 + h * 32, 32)]
    for s in range(16):
        panel_ref[:, s, :] = -flat_ref[s // 2, s % 2]
    for r in range(4):
        rows = pl.ds(r * 8, 8)
        panel_ref[rows] = panel_ref[rows] * mask_ref[r][None]


def finish_call(place, mask, diag_inv, parts, shape):
    chunks = (NG, 256, 128)
    panel, diagonal = pl.pallas_call(
        finish_kernel,
        out_shape=[
            jax.ShapeDtypeStruct(shape, jnp.float32),
            jax.ShapeDtypeStruct(chunks, jnp.float32),
        ],
        in_specs=[SMEM] + [VMEM] * 10,
        out_specs=[VMEM] * 2,
        scratch_shapes=[pltpu.VMEM((NG, 2, 32, 128), jnp.float32)],
        compiler_params=pltpu.CompilerParams(vmem_limit_bytes=8 << 20),
        cost_estimate=pl.CostEstimate(flops=1 << 18, bytes_accessed=4 << 20, transcendentals=0),
        name="finish",
    )(place, mask, diag_inv.reshape(chunks), *parts)
    return panel, diagonal.reshape(diag_inv.shape)


def per_device(ancestor, factor, diag_inv, structure):
    rows, sib, width = factor.shape
    cols = sib * width // NG
    per = sib // NG
    side = ancestor.shape[0]
    z = lax.axis_index("z")
    ylo = lax.axis_index("ylo")
    yhi = lax.axis_index("yhi")
    core = lax.axis_index("core")
    group = ylo * 4 + yhi * 2 + core
    first_row = (lax.axis_index(ROW) * 16 + lax.axis_index(COL)) * rows
    place = jnp.stack([first_row // RB, group, yhi, core, lax.axis_index("x"), z]).astype(jnp.int32)

    pieces, mask, local = pack_call(place, factor, structure, cols)
    pieces = lax.all_to_all(pieces, "z", 0, 0, tiled=True)
    near = flip_to(ancestor, RING_Y, 4, 2)
    back = flip_to(ancestor, RING_Y, 4, 3)
    own_c = flip_to(ancestor, "core", 2, 1)
    pieces, near, back, own_c = lax.optimization_barrier((pieces, near, back, own_c))
    near_c, back_c = flip_to(near, "core", 2, 1), flip_to(back, "core", 2, 1)
    half = side // 2
    far0 = flip_to(near[:half], RING_Y, 4, 3)
    far1 = flip_to(back[half:], RING_Y, 4, 2)
    pieces = turn_call(pieces).reshape(NX * NG, 2, 8, width)
    pieces = lax.all_to_all(pieces, ("x",) + GROUP, 0, 0, tiled=True)
    pieces, near_c, back_c = lax.optimization_barrier((pieces, near_c, back_c))
    ups, downs = [pieces], [pieces]
    for step in range(1, NZ // 2 + 1):
        ups.append(lax.ppermute(ups[-1], "z", shift(NZ, 1)))
        if step < NZ // 2:
            downs.append(lax.ppermute(downs[-1], "z", shift(NZ, -1)))
        if step == 1:
            ups[-1], downs[-1] = lax.optimization_barrier((ups[-1], downs[-1]))
            local = lax.all_to_all(after(local, ups[-1]), GROUP, 0, 0, tiled=True)
        elif step == 2:
            ups[-1], downs[-1], far0, far1 = lax.optimization_barrier(
                (ups[-1], downs[-1], far0, far1)
            )
        elif step == 3:
            ups[-1], downs[-1], local = lax.optimization_barrier((ups[-1], downs[-1], local))
    ring = ups + downs[:0:-1]

    far0_c, far1_c = flip_to(far0, "core", 2, 1), flip_to(far1, "core", 2, 1)
    blocks = [ancestor, own_c, near, near_c, back, back_c, far0, far0_c, far1, far1_c]
    partial = product_call(place, blocks, ring, cols)

    recv = lax.all_to_all(partial.reshape(NX, NG * rows, cols), "x", 0, 0, tiled=True)
    update, parts = reduce_call(place, recv, local, per, width)

    members = NZ * NX
    update = update.reshape(members, per * width // members, width)
    update = lax.all_to_all(update, ("z", "x"), 0, 0, tiled=True).sum(0)
    update = jnp.broadcast_to(update[None], (members,) + update.shape)
    update = lax.all_to_all(update, ("z", "x"), 0, 0, tiled=True)
    around = [update.reshape(per * width, width)]
    around = [
        jnp.concatenate(around + [part.reshape(4 * rows, width)], 0) for part in parts
    ]
    around = [flip_to(part, RING_Y, 4, k) if k else part for k, part in enumerate(around)]
    around = around + [flip_to(part, "core", 2, 1) for part in around]
    return finish_call(place, mask, diag_inv, around, factor.shape)


def solution(mesh):
    fine = Mesh(mesh.devices.reshape(8, 2, 2, 4, 2), AXES)
    return jax.shard_map(
        per_device,
        mesh=fine,
        in_specs=(P(ROW, COL), P(ROW + COL, None, None), P(), P()),
        out_specs=(P(ROW + COL, None, None), P()),
        check_vma=False,
    )
```

```python
import jax
import jax.numpy as jnp
from jax import lax
from jax.experimental import pallas as pl
from jax.experimental.pallas import tpu as pltpu
from jax.sharding import Mesh, PartitionSpec as P

RB = 8
AXES = ("z", "ylo", "yhi", "x", "core")
ROW = ("z", "ylo")
COL = ("yhi", "x", "core")
RING_Y = ("ylo", "yhi")
GROUP = ("ylo", "yhi", "core")
NZ, NX, NG = 8, 4, 8


def shift(count, step):
    return [(i, (i + step) % count) for i in range(count)]


def flip_to(value, axes, count, bits):
    return lax.ppermute(value, axes, [(j, j ^ bits) for j in range(count)])


def after(value, *others):
    return lax.optimization_barrier((value,) + others)[0]


VMEM = pl.BlockSpec(memory_space=pltpu.VMEM)
SMEM = pl.BlockSpec(memory_space=pltpu.SMEM)


def split(value):
    high = value.astype(jnp.bfloat16)
    return high, (value - high.astype(jnp.float32)).astype(jnp.bfloat16)


def product_kernel(place_ref, *refs):
    blocks, ring, out_ref = refs[:10], refs[10:18], refs[18]
    flat_ref, high_ref, low_ref = refs[19:]
    own, own_c, near, near_c, back, back_c, far0, far0_c, far1, far1_c = blocks
    for k in range(NZ):
        source = lax.bitwise_and(place_ref[5] + (NZ - k), NZ - 1)
        for rel in range(2):
            for yl in range(2):
                tiles = [
                    ring[k][x * 8 + yl * 4 + yh * 2 + c, rel]
                    for yh in range(2)
                    for x in range(NX)
                    for c in range(2)
                ]
                at = rel * 2 + (place_ref[3] ^ yl)
                flat_ref[source & 1, at, :, source >> 1] = jnp.stack(tiles)
    depth = 512
    for i in range(4):
        both = []
        for h in range(2):
            part = flat_ref[h, i]
            both.append(part.reshape(depth, 128))
        high, low = split(jnp.concatenate(both, 1))
        high_ref[i], low_ref[i] = high, low
    for a in range(2):
        for yh in range(2):
            rows = pl.ds(yh * 256, 256)
            if a:
                parts = [near[rows], near_c[rows], back[rows], back_c[rows]]
            else:
                far, far_c = ((far0, far0_c), (far1, far1_c))[yh]
                parts = [own[rows], own_c[rows], far[...], far_c[...]]
            total = jnp.zeros((256, 256), jnp.float32)
            for i, part in enumerate(parts):
                high, low = split(part)
                for left, right in ((high, high_ref), (high, low_ref), (low, high_ref)):
                    total += jnp.dot(left, right[i], preferred_element_type=jnp.float32)
            for x in range(NX):
                out_ref[x, a, yh] = total[x * 64 : (x + 1) * 64]


def product_call(place, blocks, ring, cols):
    return pl.pallas_call(
        product_kernel,
        out_shape=jax.ShapeDtypeStruct((NX, 2, 2, 64, cols), jnp.float32),
        in_specs=[SMEM] + [VMEM] * (len(blocks) + len(ring)),
        out_specs=VMEM,
        scratch_shapes=[
            pltpu.VMEM((2, 4, 16, 4, 8, 128), jnp.float32),
            pltpu.VMEM((4, 512, cols), jnp.bfloat16),
            pltpu.VMEM((4, 512, cols), jnp.bfloat16),
        ],
        compiler_params=pltpu.CompilerParams(vmem_limit_bytes=20 << 20),
        cost_estimate=pl.CostEstimate(
            flops=6 * 1024 * 2048 * 256, bytes_accessed=12 << 20, transcendentals=0
        ),
        name="product",
    )(place, *blocks, *ring)


def pack_kernel(place_ref, factor_ref, structure_ref, pieces_ref, mask_ref, rows_ref, masked_ref):
    structure = structure_ref[...]
    for r in range(4):
        hit = jnp.where(structure == place_ref[0] + r, 1.0, 0.0).astype(jnp.float32)
        mask = jnp.max(hit, axis=1, keepdims=True)
        mask = jnp.broadcast_to(mask, mask_ref.shape[1:])
        mask_ref[r] = mask
        rows = pl.ds(r * 8, 8)
        masked_ref[rows] = factor_ref[rows] * mask[None]
        for s in range(16):
            pieces_ref[r * 2 + s % 2, s // 2] = masked_ref[rows, s, :]
    for s in range(16):
        rows_ref[s // 2, :, pl.ds(s % 2 * 128, 128)] = masked_ref[:, s, :]


def pack_call(place, factor, structure, cols):
    rows, sib, width = factor.shape
    return pl.pallas_call(
        pack_kernel,
        out_shape=[
            jax.ShapeDtypeStruct((NZ, NG, 8, width), jnp.float32),
            jax.ShapeDtypeStruct((4, sib, width), jnp.float32),
            jax.ShapeDtypeStruct((NG, rows, cols), jnp.float32),
        ],
        in_specs=[SMEM, VMEM, VMEM],
        out_specs=[VMEM] * 3,
        scratch_shapes=[pltpu.VMEM((rows, sib, width), jnp.float32)],
        compiler_params=pltpu.CompilerParams(vmem_limit_bytes=4 << 20),
        cost_estimate=pl.CostEstimate(flops=1 << 16, bytes_accessed=1 << 20, transcendentals=0),
        name="pack",
    )(place, factor, structure)


def turn_kernel(in_ref, out_ref):
    for g in range(NG):
        for rel in range(2):
            first = ((g >> 1 & 1) ^ rel) * NX
            out_ref[:, g, rel] = in_ref[first : first + NX, g]


def turn_call(pieces):
    shape = (NX, NG, 2) + pieces.shape[2:]
    return pl.pallas_call(
        turn_kernel,
        out_shape=jax.ShapeDtypeStruct(shape, jnp.float32),
        in_specs=[VMEM],
        out_specs=VMEM,
        compiler_params=pltpu.CompilerParams(vmem_limit_bytes=2 << 20),
        cost_estimate=pl.CostEstimate(flops=0, bytes_accessed=1 << 19, transcendentals=0),
        name="turn",
    )(pieces)


def block_of(place_ref, k):
    return (k >> 2) * 4 + (place_ref[2] ^ (k >> 1 & 1)) * 2 + (place_ref[3] ^ (k & 1))


def reduce_kernel(place_ref, recv_ref, local_ref, *refs):
    update_ref, outs, sum_ref, rows_ref = refs[0], refs[1:5], refs[5], refs[6]
    total = recv_ref[0] + recv_ref[1] + recv_ref[2] + recv_ref[3]
    sum_ref[...] = total.reshape(sum_ref.shape)
    for k in range(NG):
        at = block_of(place_ref, k)
        rows_ref[at] = local_ref[place_ref[1] ^ k]
        for h in range(2):
            outs[k >> 1][1 - k % 2, h] = sum_ref[at, :, pl.ds(h * 128, 128)]
    left = rows_ref[...].reshape(total.shape)
    for s in range(2):
        lanes = slice(s * 128, (s + 1) * 128)
        update_ref[s] = lax.dot_general(
            left[:, lanes],
            total[:, lanes],
            (((0,), (0,)), ((), ())),
            precision=lax.Precision.HIGHEST,
            preferred_element_type=jnp.float32,
        )


def reduce_call(place, recv, local, per, width):
    rows = local.shape[1]
    piece = jax.ShapeDtypeStruct((2, per, rows, width), jnp.float32)
    whole = jax.ShapeDtypeStruct((per, width, width), jnp.float32)
    block = pltpu.VMEM(local.shape, jnp.float32)
    out = pl.pallas_call(
        reduce_kernel,
        out_shape=[whole] + [piece] * 4,
        in_specs=[SMEM, VMEM, VMEM],
        out_specs=[VMEM] * 5,
        scratch_shapes=[block, block],
        compiler_params=pltpu.CompilerParams(vmem_limit_bytes=8 << 20),
        cost_estimate=pl.CostEstimate(flops=1 << 25, bytes_accessed=2 << 20, transcendentals=0),
        name="reduce",
    )(place, recv, local)
    return out[0], out[1:]


def finish_kernel(place_ref, mask_ref, diag_ref, *refs):
    parts, panel_ref, out_ref, flat_ref = refs[:8], refs[8], refs[9], refs[10]
    for c in range(2):
        for k in range(4):
            part = parts[c * 4 + k]
            at = place_ref[1] ^ (k * 2 + c)
            out_ref[at] = diag_ref[at] + part[pl.ds(0, 256)]
            for h in range(2):
                flat_ref[at, h] = part[pl.ds(256 + (1 - c) * 64 + h * 32, 32)]
    for s in range(16):
        panel_ref[:, s, :] = -flat_ref[s // 2, s % 2]
    for r in range(4):
        rows = pl.ds(r * 8, 8)
        panel_ref[rows] = panel_ref[rows] * mask_ref[r][None]


def finish_call(place, mask, diag_inv, parts, shape):
    chunks = (NG, 256, 128)
    panel, diagonal = pl.pallas_call(
        finish_kernel,
        out_shape=[
            jax.ShapeDtypeStruct(shape, jnp.float32),
            jax.ShapeDtypeStruct(chunks, jnp.float32),
        ],
        in_specs=[SMEM] + [VMEM] * 10,
        out_specs=[VMEM] * 2,
        scratch_shapes=[pltpu.VMEM((NG, 2, 32, 128), jnp.float32)],
        compiler_params=pltpu.CompilerParams(vmem_limit_bytes=8 << 20),
        cost_estimate=pl.CostEstimate(flops=1 << 18, bytes_accessed=4 << 20, transcendentals=0),
        name="finish",
    )(place, mask, diag_inv.reshape(chunks), *parts)
    return panel, diagonal.reshape(diag_inv.shape)


def per_device(ancestor, factor, diag_inv, structure):
    rows, sib, width = factor.shape
    cols = sib * width // NG
    per = sib // NG
    side = ancestor.shape[0]
    z = lax.axis_index("z")
    ylo = lax.axis_index("ylo")
    yhi = lax.axis_index("yhi")
    core = lax.axis_index("core")
    group = ylo * 4 + yhi * 2 + core
    first_row = (lax.axis_index(ROW) * 16 + lax.axis_index(COL)) * rows
    place = jnp.stack([first_row // RB, group, yhi, core, lax.axis_index("x"), z]).astype(jnp.int32)

    pieces, mask, local = pack_call(place, factor, structure, cols)
    pieces = lax.all_to_all(pieces, "z", 0, 0, tiled=True)
    near = flip_to(ancestor, RING_Y, 4, 2)
    back = flip_to(ancestor, RING_Y, 4, 3)
    own_c = flip_to(ancestor, "core", 2, 1)
    local = lax.all_to_all(after(local, pieces), GROUP, 0, 0, tiled=True)
    pieces, near, back, own_c, local = lax.optimization_barrier(
        (pieces, near, back, own_c, local)
    )
    near_c, back_c = flip_to(near, "core", 2, 1), flip_to(back, "core", 2, 1)
    half = side // 2
    far0 = flip_to(near[:half], RING_Y, 4, 3)
    far1 = flip_to(back[half:], RING_Y, 4, 2)
    pieces = turn_call(pieces).reshape(NX * NG, 2, 8, width)
    pieces = lax.all_to_all(pieces, ("x",) + GROUP, 0, 0, tiled=True)
    pieces, near_c, back_c = lax.optimization_barrier((pieces, near_c, back_c))
    ups, downs = [pieces], [pieces]
    for step in range(1, NZ // 2 + 1):
        ups.append(lax.ppermute(ups[-1], "z", shift(NZ, 1)))
        if step < NZ // 2:
            downs.append(lax.ppermute(downs[-1], "z", shift(NZ, -1)))
        if step == 2:
            ups[-1], downs[-1], far0, far1 = lax.optimization_barrier(
                (ups[-1], downs[-1], far0, far1)
            )
        elif step < NZ // 2:
            ups[-1], downs[-1] = lax.optimization_barrier((ups[-1], downs[-1]))
    ring = ups + downs[:0:-1]

    far0_c, far1_c = flip_to(far0, "core", 2, 1), flip_to(far1, "core", 2, 1)
    blocks = [ancestor, own_c, near, near_c, back, back_c, far0, far0_c, far1, far1_c]
    partial = product_call(place, blocks, ring, cols)

    recv = lax.all_to_all(partial.reshape(NX, NG * rows, cols), "x", 0, 0, tiled=True)
    update, parts = reduce_call(place, recv, local, per, width)

    members = NZ * NX
    update = update.reshape(members, per * width // members, width)
    update = lax.all_to_all(update, ("z", "x"), 0, 0, tiled=True).sum(0)
    update = jnp.broadcast_to(update[None], (members,) + update.shape)
    update = lax.all_to_all(update, ("z", "x"), 0, 0, tiled=True)
    around = [update.reshape(per * width, width)]
    around = [
        jnp.concatenate(around + [part.reshape(4 * rows, width)], 0) for part in parts
    ]
    around = [flip_to(part, RING_Y, 4, k) if k else part for k, part in enumerate(around)]
    around = around + [flip_to(part, "core", 2, 1) for part in around]
    return finish_call(place, mask, diag_inv, around, factor.shape)


def solution(mesh):
    fine = Mesh(mesh.devices.reshape(8, 2, 2, 4, 2), AXES)
    return jax.shard_map(
        per_device,
        mesh=fine,
        in_specs=(P(ROW, COL), P(ROW + COL, None, None), P(), P()),
        out_specs=(P(ROW + COL, None, None), P()),
        check_vma=False,
    )
```

```python
import jax
import jax.numpy as jnp
from jax import lax
from jax.experimental import pallas as pl
from jax.experimental.pallas import tpu as pltpu
from jax.sharding import Mesh, PartitionSpec as P

RB = 8
AXES = ("z", "ylo", "yhi", "x", "core")
ROW = ("z", "ylo")
COL = ("yhi", "x", "core")
RING_Y = ("ylo", "yhi")
GROUP = ("ylo", "yhi", "core")
NZ, NX, NG = 8, 4, 8


def shift(count, step):
    return [(i, (i + step) % count) for i in range(count)]


def flip_to(value, axes, count, bits):
    return lax.ppermute(value, axes, [(j, j ^ bits) for j in range(count)])


def after(value, *others):
    return lax.optimization_barrier((value,) + others)[0]


VMEM = pl.BlockSpec(memory_space=pltpu.VMEM)
SMEM = pl.BlockSpec(memory_space=pltpu.SMEM)


def split(value):
    high = value.astype(jnp.bfloat16)
    return high, (value - high.astype(jnp.float32)).astype(jnp.bfloat16)


def product_kernel(place_ref, *refs):
    blocks, ring, out_ref = refs[:10], refs[10:18], refs[18]
    flat_ref, high_ref, low_ref = refs[19:]
    own, own_c, near, near_c, back, back_c, far0, far0_c, far1, far1_c = blocks
    for k in range(NZ):
        source = lax.bitwise_and(place_ref[5] + (NZ - k), NZ - 1)
        for rel in range(2):
            for yl in range(2):
                tiles = [
                    ring[k][x * 8 + yl * 4 + yh * 2 + c, rel]
                    for yh in range(2)
                    for x in range(NX)
                    for c in range(2)
                ]
                at = rel * 2 + (place_ref[3] ^ yl)
                flat_ref[source & 1, at, :, source >> 1] = jnp.stack(tiles)
    depth = 512
    for i in range(4):
        both = []
        for h in range(2):
            part = flat_ref[h, i]
            both.append(part.reshape(depth, 128))
        high, low = split(jnp.concatenate(both, 1))
        high_ref[i], low_ref[i] = high, low
    for a in range(2):
        for yh in range(2):
            rows = pl.ds(yh * 256, 256)
            if a:
                parts = [near[rows], near_c[rows], back[rows], back_c[rows]]
            else:
                far, far_c = ((far0, far0_c), (far1, far1_c))[yh]
                parts = [own[rows], own_c[rows], far[...], far_c[...]]
            total = jnp.zeros((256, 256), jnp.float32)
            for i, part in enumerate(parts):
                high, low = split(part)
                for left, right in ((high, high_ref), (high, low_ref), (low, high_ref)):
                    total += jnp.dot(left, right[i], preferred_element_type=jnp.float32)
            for x in range(NX):
                out_ref[x, a, yh] = total[x * 64 : (x + 1) * 64]


def product_call(place, blocks, ring, cols):
    return pl.pallas_call(
        product_kernel,
        out_shape=jax.ShapeDtypeStruct((NX, 2, 2, 64, cols), jnp.float32),
        in_specs=[SMEM] + [VMEM] * (len(blocks) + len(ring)),
        out_specs=VMEM,
        scratch_shapes=[
            pltpu.VMEM((2, 4, 16, 4, 8, 128), jnp.float32),
            pltpu.VMEM((4, 512, cols), jnp.bfloat16),
            pltpu.VMEM((4, 512, cols), jnp.bfloat16),
        ],
        compiler_params=pltpu.CompilerParams(vmem_limit_bytes=20 << 20),
        cost_estimate=pl.CostEstimate(
            flops=6 * 1024 * 2048 * 256, bytes_accessed=12 << 20, transcendentals=0
        ),
        name="product",
    )(place, *blocks, *ring)


def pack_kernel(place_ref, factor_ref, structure_ref, pieces_ref, mask_ref, rows_ref, masked_ref):
    structure = structure_ref[...]
    for r in range(4):
        hit = jnp.where(structure == place_ref[0] + r, 1.0, 0.0).astype(jnp.float32)
        mask = jnp.max(hit, axis=1, keepdims=True)
        mask = jnp.broadcast_to(mask, mask_ref.shape[1:])
        mask_ref[r] = mask
        rows = pl.ds(r * 8, 8)
        masked_ref[rows] = factor_ref[rows] * mask[None]
        for s in range(16):
            pieces_ref[r * 2 + s % 2, s // 2] = masked_ref[rows, s, :]
    for s in range(16):
        rows_ref[s // 2, :, pl.ds(s % 2 * 128, 128)] = masked_ref[:, s, :]


def pack_call(place, factor, structure, cols):
    rows, sib, width = factor.shape
    return pl.pallas_call(
        pack_kernel,
        out_shape=[
            jax.ShapeDtypeStruct((NZ, NG, 8, width), jnp.float32),
            jax.ShapeDtypeStruct((4, sib, width), jnp.float32),
            jax.ShapeDtypeStruct((NG, rows, cols), jnp.float32),
        ],
        in_specs=[SMEM, VMEM, VMEM],
        out_specs=[VMEM] * 3,
        scratch_shapes=[pltpu.VMEM((rows, sib, width), jnp.float32)],
        compiler_params=pltpu.CompilerParams(vmem_limit_bytes=4 << 20),
        cost_estimate=pl.CostEstimate(flops=1 << 16, bytes_accessed=1 << 20, transcendentals=0),
        name="pack",
    )(place, factor, structure)


def turn_kernel(in_ref, out_ref):
    for g in range(NG):
        for rel in range(2):
            first = ((g >> 1 & 1) ^ rel) * NX
            out_ref[:, g, rel] = in_ref[first : first + NX, g]


def turn_call(pieces):
    shape = (NX, NG, 2) + pieces.shape[2:]
    return pl.pallas_call(
        turn_kernel,
        out_shape=jax.ShapeDtypeStruct(shape, jnp.float32),
        in_specs=[VMEM],
        out_specs=VMEM,
        compiler_params=pltpu.CompilerParams(vmem_limit_bytes=2 << 20),
        cost_estimate=pl.CostEstimate(flops=0, bytes_accessed=1 << 19, transcendentals=0),
        name="turn",
    )(pieces)


def block_of(place_ref, k):
    return (k >> 2) * 4 + (place_ref[2] ^ (k >> 1 & 1)) * 2 + (place_ref[3] ^ (k & 1))


def reduce_kernel(place_ref, recv_ref, local_ref, *refs):
    update_ref, outs, sum_ref, rows_ref = refs[0], refs[1:5], refs[5], refs[6]
    total = recv_ref[0] + recv_ref[1] + recv_ref[2] + recv_ref[3]
    sum_ref[...] = total.reshape(sum_ref.shape)
    for k in range(NG):
        at = block_of(place_ref, k)
        rows_ref[at] = local_ref[place_ref[1] ^ k]
        for h in range(2):
            outs[k >> 1][1 - k % 2, h] = sum_ref[at, :, pl.ds(h * 128, 128)]
    left = rows_ref[...].reshape(total.shape)
    for s in range(2):
        lanes = slice(s * 128, (s + 1) * 128)
        update_ref[s] = lax.dot_general(
            left[:, lanes],
            total[:, lanes],
            (((0,), (0,)), ((), ())),
            precision=lax.Precision.HIGHEST,
            preferred_element_type=jnp.float32,
        )


def reduce_call(place, recv, local, per, width):
    rows = local.shape[1]
    piece = jax.ShapeDtypeStruct((2, per, rows, width), jnp.float32)
    whole = jax.ShapeDtypeStruct((per, width, width), jnp.float32)
    block = pltpu.VMEM(local.shape, jnp.float32)
    out = pl.pallas_call(
        reduce_kernel,
        out_shape=[whole] + [piece] * 4,
        in_specs=[SMEM, VMEM, VMEM],
        out_specs=[VMEM] * 5,
        scratch_shapes=[block, block],
        compiler_params=pltpu.CompilerParams(vmem_limit_bytes=8 << 20),
        cost_estimate=pl.CostEstimate(flops=1 << 25, bytes_accessed=2 << 20, transcendentals=0),
        name="reduce",
    )(place, recv, local)
    return out[0], out[1:]


def finish_kernel(place_ref, mask_ref, diag_ref, *refs):
    parts, early = refs[:8], refs[8:10]
    panel_ref, out_ref, flat_ref = refs[10:]
    for c in range(2):
        for k in range(4):
            part = parts[c * 4 + k]
            at = place_ref[1] ^ (k * 2 + c)
            out_ref[at] = diag_ref[at] + part[pl.ds(0, 256)]
            for h in range(2):
                first = (1 - c) * 64 + h * 32
                if k == 1:
                    flat_ref[at, h] = early[c][pl.ds(first, 32)]
                else:
                    flat_ref[at, h] = part[pl.ds(256 + first, 32)]
    for s in range(16):
        panel_ref[:, s, :] = -flat_ref[s // 2, s % 2]
    for r in range(4):
        rows = pl.ds(r * 8, 8)
        panel_ref[rows] = panel_ref[rows] * mask_ref[r][None]


def finish_call(place, mask, diag_inv, parts, shape):
    chunks = (NG, 256, 128)
    panel, diagonal = pl.pallas_call(
        finish_kernel,
        out_shape=[
            jax.ShapeDtypeStruct(shape, jnp.float32),
            jax.ShapeDtypeStruct(chunks, jnp.float32),
        ],
        in_specs=[SMEM] + [VMEM] * 12,
        out_specs=[VMEM] * 2,
        scratch_shapes=[pltpu.VMEM((NG, 2, 32, 128), jnp.float32)],
        compiler_params=pltpu.CompilerParams(vmem_limit_bytes=8 << 20),
        cost_estimate=pl.CostEstimate(flops=1 << 18, bytes_accessed=4 << 20, transcendentals=0),
        name="finish",
    )(place, mask, diag_inv.reshape(chunks), *parts)
    return panel, diagonal.reshape(diag_inv.shape)


def per_device(ancestor, factor, diag_inv, structure):
    rows, sib, width = factor.shape
    cols = sib * width // NG
    per = sib // NG
    side = ancestor.shape[0]
    z = lax.axis_index("z")
    ylo = lax.axis_index("ylo")
    yhi = lax.axis_index("yhi")
    core = lax.axis_index("core")
    group = ylo * 4 + yhi * 2 + core
    first_row = (lax.axis_index(ROW) * 16 + lax.axis_index(COL)) * rows
    place = jnp.stack([first_row // RB, group, yhi, core, lax.axis_index("x"), z]).astype(jnp.int32)

    pieces, mask, local = pack_call(place, factor, structure, cols)
    pieces = lax.all_to_all(pieces, "z", 0, 0, tiled=True)
    near = flip_to(ancestor, RING_Y, 4, 2)
    back = flip_to(ancestor, RING_Y, 4, 3)
    own_c = flip_to(ancestor, "core", 2, 1)
    local = lax.all_to_all(after(local, pieces), GROUP, 0, 0, tiled=True)
    pieces, near, back, own_c, local = lax.optimization_barrier(
        (pieces, near, back, own_c, local)
    )
    near_c, back_c = flip_to(near, "core", 2, 1), flip_to(back, "core", 2, 1)
    half = side // 2
    far0 = flip_to(near[:half], RING_Y, 4, 3)
    far1 = flip_to(back[half:], RING_Y, 4, 2)
    pieces = turn_call(pieces).reshape(NX * NG, 2, 8, width)
    pieces = lax.all_to_all(pieces, ("x",) + GROUP, 0, 0, tiled=True)
    pieces, near_c, back_c = lax.optimization_barrier((pieces, near_c, back_c))
    ups, downs = [pieces], [pieces]
    for step in range(1, NZ // 2 + 1):
        ups.append(lax.ppermute(ups[-1], "z", shift(NZ, 1)))
        if step < NZ // 2:
            downs.append(lax.ppermute(downs[-1], "z", shift(NZ, -1)))
        if step == 2:
            ups[-1], downs[-1], far0, far1 = lax.optimization_barrier(
                (ups[-1], downs[-1], far0, far1)
            )
        elif step < NZ // 2:
            ups[-1], downs[-1] = lax.optimization_barrier((ups[-1], downs[-1]))
    ring = ups + downs[:0:-1]

    far0_c, far1_c = flip_to(far0, "core", 2, 1), flip_to(far1, "core", 2, 1)
    blocks = [ancestor, own_c, near, near_c, back, back_c, far0, far0_c, far1, far1_c]
    partial = product_call(place, blocks, ring, cols)

    recv = lax.all_to_all(partial.reshape(NX, NG * rows, cols), "x", 0, 0, tiled=True)
    update, parts = reduce_call(place, recv, local, per, width)

    members = NZ * NX
    update = update.reshape(members, per * width // members, width)
    update = lax.all_to_all(update, ("z", "x"), 0, 0, tiled=True).sum(0)
    early = flip_to(parts[1].reshape(4 * rows, width), RING_Y, 4, 1)
    update, early = lax.optimization_barrier((update, early))
    early = [early, flip_to(early, "core", 2, 1)]
    update = jnp.broadcast_to(update[None], (members,) + update.shape)
    update = lax.all_to_all(update, ("z", "x"), 0, 0, tiled=True)
    around = [update.reshape(per * width, width)]
    around = [
        around[0] if k == 1 else jnp.concatenate(around + [part.reshape(4 * rows, width)], 0)
        for k, part in enumerate(parts)
    ]
    around = [flip_to(part, RING_Y, 4, k) if k else part for k, part in enumerate(around)]
    around = around + [flip_to(part, "core", 2, 1) for part in around]
    return finish_call(place, mask, diag_inv, around + early, factor.shape)


def solution(mesh):
    fine = Mesh(mesh.devices.reshape(8, 2, 2, 4, 2), AXES)
    return jax.shard_map(
        per_device,
        mesh=fine,
        in_specs=(P(ROW, COL), P(ROW + COL, None, None), P(), P()),
        out_specs=(P(ROW + COL, None, None), P()),
        check_vma=False,
    )
```
